32 devices in a mesh: grp: 1, freq: 32 (over z, y, x, core), pair: 1.
Axes of the slice: x: 2, y: 2, z: 4, core: 2. Of those that a mesh axis runs over, the one named last changes fastest.
Arguments:
- spectra: bfloat16 [96, 1024, 2, 512], P(('grp', 'pair'), 'freq'), may hold values from -6 to 6
- valid: int32 [96, 512], P(('grp', 'pair')), may hold values 0 or 1
- ref_spectra: bfloat16 [96, 1024, 2, 256], P(('grp', 'pair'), 'freq'), may hold values from -6 to 6
- ref_valid: int32 [96, 256], P(('grp', 'pair')), may hold values 0 or 1
Outputs:
- xcorr: float32 [401, 512, 256], P('grp', ('freq', 'pair'))
The draws below stay inside these ranges and needn't reach their ends.
All inputs are finite; a program needn't handle non-finite values. No bound on the sum of `valid` or of `ref_valid` on one device may be relied on, other than what follows from the above.
Results may differ from the reference program's by a relative error of at most 0.0054.
Values may be sent and summed in bfloat16 or wider, within the bound.
A program may use at most 192 MiB of HBM per device.

```python
import jax
import jax.numpy as jnp
from jax import lax

S = 512
F = 1024
LAGS = 401
REACH = 10
SRC = 256
W = 96


def plant(drawn, rng, least, top_value):
    index_at = [jax.random.randint(jax.random.fold_in(rng, axis), (), 0, length) for axis, length in enumerate(drawn.shape)]
    widest = drawn.shape.index(max(drawn.shape))
    beside = index_at[:widest] + [(index_at[widest] + 1) % drawn.shape[widest]] + index_at[widest + 1:]
    return drawn.at[tuple(index_at)].set(least).at[tuple(beside)].set(top_value)


def shard_levels(rng, shape, cuts, low, top_value):
    def one(axis_at, parts):
        heights = jax.random.uniform(jax.random.fold_in(jax.random.fold_in(rng, 6), axis_at), (parts,), jnp.float32, low / len(cuts), top_value / len(cuts))
        return jnp.repeat(jnp.exp(heights), shape[axis_at] // parts).reshape((-1,) + (1,) * (len(shape) - axis_at - 1))

    gain = one(*cuts[0])
    for cut in cuts[1:]:
        gain = gain * one(*cut)
    return gain


def scatter_about(key, extent, deviation, reach, pieces=(), kind=jnp.bfloat16):
    drawn = jax.random.normal(key, extent, jnp.float32) * deviation
    if len(pieces) > 0:
        drawn = shard_levels(key, extent, pieces, -0.22, 0.18) * drawn
    return jnp.clip(drawn, min=-reach, max=reach).astype(kind)


def setup_inputs(seed: int = 0, part: int = 0) -> dict:
    seeds = jax.random.split(jax.random.key(seed), 5)
    part_splits = jax.random.split(jax.random.fold_in(seeds[4], part), 5)
    return {
        "spectra": scatter_about(part_splits[0], (W, F, 2, S), 1.0, 6.0, ((1, 32),)),
        "valid": plant((jax.random.randint(part_splits[1], (W, S), 0, 4) < 3).astype(jnp.int32), jax.random.fold_in(part_splits[1], 1), 0, 1),
        "ref_spectra": scatter_about(part_splits[2], (W, F, 2, SRC), 1.0, 6.0, ((1, 32),)),
        "ref_valid": plant((jax.random.randint(part_splits[3], (W, SRC), 0, 4) < 3).astype(jnp.int32), jax.random.fold_in(part_splits[3], 1), 0, 1),
    }


water_level = 0.1
block_bins = 64

def power_of(spectra):
    real_part = spectra[:, :, 0].astype(jnp.float32)
    imag_part = spectra[:, :, 1].astype(jnp.float32)
    return real_part * real_part + imag_part * imag_part

def lag_table(first_bin, bin_total):
    bin_index = first_bin + jnp.arange(bin_total, dtype=jnp.int32)
    offsets = jnp.arange(LAGS, dtype=jnp.int32) - (LAGS - 1) // 2
    phases = jnp.mod(offsets[:, None] * bin_index[None, :], F).astype(jnp.float32) * (2.0 * jnp.pi / F)
    norm_scale = 1.0 / jnp.sqrt(jnp.float32(F))
    return jnp.stack([jnp.cos(phases) * norm_scale, -jnp.sin(phases) * norm_scale], axis=1).astype(jnp.bfloat16)

def rotated(white):
    turned = jnp.stack([-white[:, :, 1], white[:, :, 0]], axis=2)
    return jnp.concatenate([white, turned], axis=3)

def whiten(spectra, validity, padded, first_bin):
    window = lax.dynamic_slice_in_dim(padded, first_bin, block_bins + 2 * REACH, 1)
    smooth = window[:, 0:block_bins]
    for offset_bins in range(1, 2 * REACH + 1):
        smooth = smooth + window[:, offset_bins:offset_bins + block_bins]
    smooth = smooth / (2 * REACH + 1)
    spectrum = lax.dynamic_slice_in_dim(spectra, first_bin, block_bins, 1).astype(jnp.float32)
    inverse_amp = lax.rsqrt(smooth + water_level) * validity.astype(jnp.float32)[:, None, :]
    return (spectrum * inverse_amp[:, :, None, :]).astype(jnp.bfloat16)

def reference(spectra, valid, ref_spectra, ref_valid):
    stations = spectra.shape[3]
    sources = ref_spectra.shape[3]
    padding = ((0, 0), (REACH, REACH), (0, 0))
    rec_padded = jnp.pad(power_of(spectra), padding)
    ref_padded = jnp.pad(power_of(ref_spectra), padding)
    pair_count = jnp.dot(valid.astype(jnp.float32).T, ref_valid.astype(jnp.float32), precision=lax.Precision.HIGHEST)
    norm_factor = jnp.sqrt(pair_count + 1.0)

    def accumulate(summed, block_index):
        first_bin = (block_index * block_bins).astype(jnp.int32)
        rec_white = whiten(spectra, valid, rec_padded, first_bin)
        ref_white = whiten(ref_spectra, ref_valid, ref_padded, first_bin)
        ref_both = rotated(ref_white)
        cross_gram = jnp.einsum('wfcj,wfck->fjk', rec_white.astype(jnp.float32), ref_both.astype(jnp.float32), precision=lax.Precision.HIGHEST)
        stacked = (cross_gram.reshape(block_bins, stations, 2, sources) / norm_factor[None, :, None, :]).astype(jnp.bfloat16)
        lag_weights = lag_table(first_bin, block_bins)
        summed = summed + jnp.einsum('fjcs,lcf->ljs', stacked.astype(jnp.float32), lag_weights.astype(jnp.float32), precision=lax.Precision.HIGHEST)
        return (summed, None)
    summed = jnp.zeros((LAGS, stations, sources), jnp.float32)
    summed, unused = lax.scan(accumulate, summed, jnp.arange(F // block_bins, dtype=jnp.int32))
    return summed
```

```python
import functools
import math

import jax
import jax.numpy as jnp
from jax import lax
from jax.experimental import pallas as pl
from jax.experimental.pallas import tpu as pltpu
from jax.sharding import PartitionSpec as P

F = 1024
LAGS = 401
REACH = 10


water_level = 0.1


def with_halo(array, sides, width):
    for axis, dim in sides:
        count, length = (lax.axis_size(axis), array.shape[dim])
        up = [(i, (i + 1) % count) for i in range(count - 1)]
        down = [(j, i) for i, j in up]
        last = lax.slice_in_dim(array, length - width, length, axis=dim)
        first = lax.slice_in_dim(array, 0, width, axis=dim)
        before = lax.ppermute(last, axis, up)
        after = lax.ppermute(first, axis, down)
        array = jnp.concatenate([before, array, after], axis=dim)
    return array


def power_of(spectra):
    real_part = spectra[:, :, 0].astype(jnp.float32)
    imag_part = spectra[:, :, 1].astype(jnp.float32)
    return real_part * real_part + imag_part * imag_part


def half_table(first_bin, bins, devs, rows):
    column = lax.broadcasted_iota(jnp.int32, (rows, devs * 2 * bins), 1)
    lag = lax.broadcasted_iota(jnp.int32, (rows, devs * 2 * bins), 0) - (LAGS - 1) // 2
    bin_index = first_bin + column // (2 * bins) * bins + column % bins
    imag = column // bins % 2
    phases = jnp.mod(lag * bin_index, F).astype(jnp.float32) * (2.0 * jnp.pi / F)
    norm_scale = 1.0 / jnp.sqrt(jnp.float32(F))
    values = jnp.where(imag == 1, -jnp.sin(phases), jnp.cos(phases)) * norm_scale
    return values.astype(jnp.bfloat16)


def exchange_kernel(n, chunks, x_ref, w_ref, out_ref, buf, part, got, send_sem, recv_sem, part_sem, got_sem, own_sem):
    h = n // 2
    rows_chunk = x_ref.shape[1] // chunks
    depth = h * x_ref.shape[2]
    sources = x_ref.shape[3]
    lags = out_ref.shape[1]
    me = lax.axis_index("freq")
    half = lax.div(me, h)
    pos = lax.rem(me, h)
    base = half * h
    other = (1 - half) * h
    partner = other + pos

    barrier = pltpu.get_barrier_semaphore()

    @pl.loop(1, h)
    def _(k):
        pl.semaphore_signal(barrier, inc=1, device_id={"freq": base + lax.rem(pos + k, h)}, device_id_type=pl.DeviceIdType.MESH)

    pl.semaphore_signal(barrier, inc=1, device_id={"freq": partner}, device_id_type=pl.DeviceIdType.MESH)
    pl.semaphore_wait(barrier, h)

    def bins_copy(s, c, k):
        p = lax.rem(pos + k, h)
        rows = pl.ds(c * rows_chunk, rows_chunk)
        return pltpu.make_async_remote_copy(
            src_ref=x_ref.at[(other if s == 0 else base) + p, rows],
            dst_ref=buf.at[s, rows, pos],
            send_sem=send_sem.at[s, c, k],
            recv_sem=recv_sem.at[s, c, k],
            device_id={"freq": base + p},
            device_id_type=pl.DeviceIdType.MESH,
        )

    def own_copy(s):
        return pltpu.make_async_copy(x_ref.at[(other if s == 0 else base) + pos], buf.at[s, :, pos], own_sem.at[s])

    def sums_copy(c):
        rows = pl.ds(c * rows_chunk, rows_chunk)
        return pltpu.make_async_remote_copy(
            src_ref=part.at[rows],
            dst_ref=got.at[rows],
            send_sem=part_sem.at[c],
            recv_sem=got_sem.at[c],
            device_id={"freq": partner},
            device_id_type=pl.DeviceIdType.MESH,
        )

    def send_bins(s, c):
        @pl.loop(1, h)
        def _(k):
            bins_copy(s, c, k).start()

    def wait_bins(s, c):
        @pl.loop(1, h)
        def _(k):
            bins_copy(s, c, k).wait_recv()

    def to_lags(s, j):
        return jnp.dot(w_ref[...], buf[s, j].reshape(depth, sources), preferred_element_type=jnp.float32)

    own_copy(0).start()
    own_copy(1).start()
    for c in range(chunks):
        send_bins(0, c)
    own_copy(0).wait()
    for c in range(chunks):
        wait_bins(0, c)

        @pl.loop(c * rows_chunk, (c + 1) * rows_chunk)
        def _(j):
            part[j] = to_lags(0, j).astype(jnp.bfloat16)

        sums_copy(c).start()
        send_bins(1, c)
    own_copy(1).wait()
    for c in range(chunks):
        wait_bins(1, c)
        sums_copy(c).wait_recv()

        @pl.loop(c * rows_chunk, (c + 1) * rows_chunk)
        def _(j):
            total = to_lags(1, j) + got[j].astype(jnp.float32)
            out_ref[j] = total[:lags]

    for c in range(chunks):
        sums_copy(c).wait_send()
        for s in range(2):
            @pl.loop(1, h)
            def _(k):
                bins_copy(s, c, k).wait_send()


def exchange(stacked, weights):
    n, recv_local, depth, sources = stacked.shape
    rows = weights.shape[0]
    h = n // 2
    chunks = math.gcd(recv_local, 4)
    return pl.pallas_call(
        functools.partial(exchange_kernel, n, chunks),
        out_shape=jax.ShapeDtypeStruct((recv_local, LAGS, sources), jnp.float32),
        in_specs=[pl.BlockSpec(memory_space=pl.ANY), pl.BlockSpec(memory_space=pltpu.VMEM)],
        out_specs=pl.BlockSpec(memory_space=pltpu.VMEM),
        scratch_shapes=[
            pltpu.VMEM((2, recv_local, h, depth, sources), jnp.bfloat16),
            pltpu.VMEM((recv_local, rows, sources), jnp.bfloat16),
            pltpu.VMEM((recv_local, rows, sources), jnp.bfloat16),
            pltpu.SemaphoreType.DMA((2, chunks, h)),
            pltpu.SemaphoreType.DMA((2, chunks, h)),
            pltpu.SemaphoreType.DMA((chunks,)),
            pltpu.SemaphoreType.DMA((chunks,)),
            pltpu.SemaphoreType.DMA((2,)),
        ],
        compiler_params=pltpu.CompilerParams(collective_id=0, has_side_effects=True, vmem_limit_bytes=56 * 1024 * 1024),
    )(stacked, weights)


def rotated(white):
    turned = jnp.stack([-white[:, :, 1], white[:, :, 0]], axis=2)
    return jnp.concatenate([white, turned], axis=3)


def local(spectra, valid, ref_spectra, ref_valid):
    local_bins = spectra.shape[1]
    stations = spectra.shape[3]
    sources = ref_spectra.shape[3]
    freq_devs = lax.axis_size("freq")
    pair_devs = lax.axis_size("pair")
    recv_local = stations // (freq_devs * pair_devs)
    powers = jnp.concatenate([power_of(spectra), power_of(ref_spectra)], axis=2)
    padded = with_halo(powers, (("freq", 1),), REACH)
    out_bins = jnp.arange(local_bins, dtype=jnp.int32)[:, None]
    in_bins = jnp.arange(local_bins + 2 * REACH, dtype=jnp.int32)[None, :]
    band_ones = jnp.where(
        (in_bins >= out_bins) & (in_bins <= out_bins + 2 * REACH), 1.0, 0.0
    ).astype(jnp.float32)
    smooth = jnp.einsum("wks,fk->wfs", padded, band_ones, precision=lax.Precision.HIGHEST) / (
        2 * REACH + 1
    )
    inverse_amp = lax.rsqrt(smooth + water_level)
    rec_gain = inverse_amp[:, :, :stations] * valid.astype(jnp.float32)[:, None, :]
    ref_gain = inverse_amp[:, :, stations:] * ref_valid.astype(jnp.float32)[:, None, :]
    rec_white = (spectra.astype(jnp.float32) * rec_gain[:, :, None, :]).astype(jnp.bfloat16)
    ref_white = (ref_spectra.astype(jnp.float32) * ref_gain[:, :, None, :]).astype(jnp.bfloat16)
    ref_both = rotated(ref_white)
    cross_gram = jnp.einsum(
        "wfcj,wfck->fjk", rec_white, ref_both, preferred_element_type=jnp.float32
    )
    pair_count = jnp.dot(
        valid.astype(jnp.float32).T, ref_valid.astype(jnp.float32), precision=lax.Precision.HIGHEST
    )
    if pair_devs > 1:
        cross_gram = cross_gram.reshape(local_bins, freq_devs, pair_devs, recv_local, 2 * sources)
        pair_count = pair_count.reshape(1, freq_devs, pair_devs, recv_local, sources)
        cross_gram, pair_count = (
            lax.psum_scatter(cross_gram, "pair", scatter_dimension=2, tiled=True),
            lax.psum_scatter(pair_count, "pair", scatter_dimension=2, tiled=True),
        )
    cross_gram = cross_gram.reshape(local_bins, freq_devs * recv_local, 2 * sources)
    pair_count = pair_count.reshape(freq_devs * recv_local, sources)
    norm = jnp.sqrt(pair_count + 1.0)
    norm = jnp.concatenate([norm, norm], axis=1)
    stacked = (cross_gram / norm[None]).astype(jnp.bfloat16)
    stacked = jnp.stack([stacked[:, :, :sources], stacked[:, :, sources:]], axis=0)
    stacked = stacked.transpose(2, 0, 1, 3).reshape(freq_devs, recv_local, 2 * local_bins, sources)
    half_devs = freq_devs // 2
    first_bin = lax.axis_index("freq") // half_devs * (half_devs * local_bins)
    weights = half_table(first_bin, local_bins, half_devs, -(-LAGS // 16) * 16)
    return exchange(stacked, weights).transpose(1, 0, 2)


def solution(mesh):
    placed = (
        P(("grp", "pair"), "freq", None, None),
        P(("grp", "pair"), None),
        P(("grp", "pair"), "freq", None, None),
        P(("grp", "pair"), None),
    )
    return jax.shard_map(
        local,
        mesh=mesh,
        in_specs=placed,
        out_specs=P("grp", ("freq", "pair"), None),
        check_vma=False,
    )
```

```python
import functools
import math

import jax
import jax.numpy as jnp
from jax import lax
from jax.experimental import pallas as pl
from jax.experimental.pallas import tpu as pltpu
from jax.sharding import PartitionSpec as P

F = 1024
LAGS = 401
REACH = 10
LANES = 128


water_level = 0.1


def edge_powers(spectra, ref_spectra, first, width):
    parts = []
    for array in (spectra, ref_spectra):
        edge = lax.slice_in_dim(array, first, first + width, axis=1).transpose(1, 2, 0, 3).astype(jnp.float32)
        parts.append(edge[:, 0] * edge[:, 0] + edge[:, 1] * edge[:, 1])
    return jnp.concatenate(parts, axis=2)


def halo_powers(spectra, ref_spectra, axis):
    count, length = lax.axis_size(axis), spectra.shape[1]
    up = [(i, (i + 1) % count) for i in range(count - 1)]
    down = [(j, i) for i, j in up]
    last = edge_powers(spectra, ref_spectra, length - REACH, REACH)
    first = edge_powers(spectra, ref_spectra, 0, REACH)
    return lax.ppermute(last, axis, up), lax.ppermute(first, axis, down)


def gram_kernel(x_ref, y_ref, before_ref, after_ref, valid_ref, ref_valid_ref, scale_ref, out_ref, power, gram, sem):
    bins = x_ref.shape[0]
    stations = x_ref.shape[3]
    sources = y_ref.shape[3]
    block = out_ref.shape[2]
    step = pl.program_id(0)

    @pl.when(step == 0)
    def _():
        copies = (
            pltpu.make_async_copy(before_ref, power.at[pl.ds(0, REACH)], sem.at[0]),
            pltpu.make_async_copy(after_ref, power.at[pl.ds(REACH + bins, REACH)], sem.at[1]),
        )
        for copy in copies:
            copy.start()

        @pl.loop(0, bins)
        def _(f):
            for ref, columns in ((x_ref, pl.ds(0, stations)), (y_ref, pl.ds(stations, sources))):
                real_part = ref[f, 0].astype(jnp.float32)
                imag_part = ref[f, 1].astype(jnp.float32)
                power[f + REACH, :, columns] = real_part * real_part + imag_part * imag_part

        for copy in copies:
            copy.wait()

        @pl.loop(0, bins + 2 * REACH - 2)
        def _(f):
            power[f] = power[f] + power[f + 1] + power[f + 2]

    @pl.loop(0, block)
    def _(b):
        f = step * block + b
        whites = []
        for ref, mask, columns in (
            (x_ref, valid_ref, pl.ds(0, stations)),
            (y_ref, ref_valid_ref, pl.ds(stations, sources)),
        ):
            smooth = power[f, :, columns]
            for k in range(3, 2 * REACH + 1, 3):
                smooth = smooth + power[f + k, :, columns]
            gain = lax.rsqrt(smooth * (1.0 / (2 * REACH + 1)) + water_level) * mask[...]
            whites.append([ref[f, c].astype(jnp.float32) * gain for c in range(2)])
        (rec_re, rec_im), (ref_re, ref_im) = whites
        rec = jnp.concatenate([rec_re.astype(jnp.bfloat16), rec_im.astype(jnp.bfloat16)], axis=0)
        for c, pieces in enumerate(((ref_re, ref_im), (-ref_im, ref_re))):
            other = jnp.concatenate([piece.astype(jnp.bfloat16) for piece in pieces], axis=0)
            cross = lax.dot_general(rec, other, (((0,), (0,)), ((), ())), preferred_element_type=jnp.float32)
            cross = cross * scale_ref[...]
            for q in range(sources // LANES):
                gram[c * (sources // LANES) + q, pl.ds(pl.multiple_of(b * stations, stations), stations)] = cross[
                    :, q * LANES : (q + 1) * LANES
                ]

    @pl.loop(0, stations, unroll=8)
    def _(j):
        for c in range(2):
            for q in range(sources // LANES):
                rows = gram[c * (sources // LANES) + q, pl.ds(j, block, stride=stations)]
                out_ref[j, c, :, pl.ds(q * LANES, LANES)] = rows.astype(out_ref.dtype)


def cross_grams(spectra, ref_spectra, before, after, valid, ref_valid, scale, dtype):
    bins, parts, windows, stations = spectra.shape
    sources = ref_spectra.shape[3]
    block = 8
    whole = lambda shape: pl.BlockSpec(shape, lambda i: (0,) * len(shape), pipeline_mode=pl.Buffered(1))
    return pl.pallas_call(
        gram_kernel,
        grid=(bins // block,),
        out_shape=jax.ShapeDtypeStruct((stations, 2, bins, sources), dtype),
        in_specs=[
            whole(spectra.shape),
            whole(ref_spectra.shape),
            pl.BlockSpec(memory_space=pl.ANY),
            pl.BlockSpec(memory_space=pl.ANY),
            whole(valid.shape),
            whole(ref_valid.shape),
            whole(scale.shape),
        ],
        out_specs=pl.BlockSpec((stations, 2, block, sources), lambda i: (0, 0, i, 0)),
        scratch_shapes=[
            pltpu.VMEM((bins + 2 * REACH, windows, stations + sources), jnp.float32),
            pltpu.VMEM((2 * sources // LANES, block * stations, LANES), jnp.float32),
            pltpu.SemaphoreType.DMA((2,)),
        ],
        compiler_params=pltpu.CompilerParams(vmem_limit_bytes=60 * 1024 * 1024),
    )(spectra, ref_spectra, before, after, valid, ref_valid, scale)


def half_table(first_bin, bins, devs, rows):
    column = lax.broadcasted_iota(jnp.int32, (rows, devs * 2 * bins), 1)
    lag = lax.broadcasted_iota(jnp.int32, (rows, devs * 2 * bins), 0) - (LAGS - 1) // 2
    bin_index = first_bin + column // (2 * bins) * bins + column % bins
    imag = column // bins % 2
    phases = jnp.mod(lag * bin_index, F).astype(jnp.float32) * (2.0 * jnp.pi / F)
    norm_scale = 1.0 / jnp.sqrt(jnp.float32(F))
    values = jnp.where(imag == 1, -jnp.sin(phases), jnp.cos(phases)) * norm_scale
    return values.astype(jnp.bfloat16)


def exchange_kernel(n, chunks, x_ref, w_ref, out_ref, buf, part, got, send_sem, recv_sem, part_sem, got_sem, own_sem):
    h = n // 2
    rows_chunk = x_ref.shape[1] // chunks
    depth = h * x_ref.shape[2]
    sources = x_ref.shape[3]
    lags = out_ref.shape[1]
    me = lax.axis_index("freq")
    half = lax.div(me, h)
    pos = lax.rem(me, h)
    base = half * h
    other = (1 - half) * h
    partner = other + pos

    barrier = pltpu.get_barrier_semaphore()

    @pl.loop(1, h)
    def _(k):
        pl.semaphore_signal(barrier, inc=1, device_id={"freq": base + lax.rem(pos + k, h)}, device_id_type=pl.DeviceIdType.MESH)

    pl.semaphore_signal(barrier, inc=1, device_id={"freq": partner}, device_id_type=pl.DeviceIdType.MESH)
    pl.semaphore_wait(barrier, h)

    def bins_copy(s, c, k):
        p = lax.rem(pos + k, h)
        rows = pl.ds(c * rows_chunk, rows_chunk)
        return pltpu.make_async_remote_copy(
            src_ref=x_ref.at[(other if s == 0 else base) + p, rows],
            dst_ref=buf.at[s, rows, pos],
            send_sem=send_sem.at[s, c, k],
            recv_sem=recv_sem.at[s, c, k],
            device_id={"freq": base + p},
            device_id_type=pl.DeviceIdType.MESH,
        )

    def own_copy(s):
        return pltpu.make_async_copy(x_ref.at[(other if s == 0 else base) + pos], buf.at[s, :, pos], own_sem.at[s])

    def sums_copy(c):
        rows = pl.ds(c * rows_chunk, rows_chunk)
        return pltpu.make_async_remote_copy(
            src_ref=part.at[rows],
            dst_ref=got.at[rows],
            send_sem=part_sem.at[c],
            recv_sem=got_sem.at[c],
            device_id={"freq": partner},
            device_id_type=pl.DeviceIdType.MESH,
        )

    def send_bins(s, c):
        @pl.loop(1, h)
        def _(k):
            bins_copy(s, c, k).start()

    def wait_bins(s, c):
        @pl.loop(1, h)
        def _(k):
            bins_copy(s, c, k).wait_recv()

    def to_lags(s, j):
        return jnp.dot(w_ref[...], buf[s, j].reshape(depth, sources), preferred_element_type=jnp.float32)

    own_copy(0).start()
    own_copy(1).start()
    for c in range(chunks):
        send_bins(0, c)
    own_copy(0).wait()
    for c in range(chunks):
        wait_bins(0, c)

        @pl.loop(c * rows_chunk, (c + 1) * rows_chunk)
        def _(j):
            part[j] = to_lags(0, j).astype(jnp.bfloat16)

        sums_copy(c).start()
        send_bins(1, c)
    own_copy(1).wait()
    for c in range(chunks):
        wait_bins(1, c)
        sums_copy(c).wait_recv()

        @pl.loop(c * rows_chunk, (c + 1) * rows_chunk)
        def _(j):
            total = to_lags(1, j) + got[j].astype(jnp.float32)
            out_ref[j] = total[:lags]

    for c in range(chunks):
        sums_copy(c).wait_send()
        for s in range(2):
            @pl.loop(1, h)
            def _(k):
                bins_copy(s, c, k).wait_send()


def exchange(stacked, weights):
    n, recv_local, depth, sources = stacked.shape
    rows = weights.shape[0]
    h = n // 2
    chunks = math.gcd(recv_local, 4)
    return pl.pallas_call(
        functools.partial(exchange_kernel, n, chunks),
        out_shape=jax.ShapeDtypeStruct((recv_local, LAGS, sources), jnp.float32),
        in_specs=[pl.BlockSpec(memory_space=pl.ANY), pl.BlockSpec(memory_space=pltpu.VMEM)],
        out_specs=pl.BlockSpec(memory_space=pltpu.VMEM),
        scratch_shapes=[
            pltpu.VMEM((2, recv_local, h, depth, sources), jnp.bfloat16),
            pltpu.VMEM((recv_local, rows, sources), jnp.bfloat16),
            pltpu.VMEM((recv_local, rows, sources), jnp.bfloat16),
            pltpu.SemaphoreType.DMA((2, chunks, h)),
            pltpu.SemaphoreType.DMA((2, chunks, h)),
            pltpu.SemaphoreType.DMA((chunks,)),
            pltpu.SemaphoreType.DMA((chunks,)),
            pltpu.SemaphoreType.DMA((2,)),
        ],
        compiler_params=pltpu.CompilerParams(collective_id=0, has_side_effects=True, vmem_limit_bytes=56 * 1024 * 1024),
    )(stacked, weights)


def local(spectra, valid, ref_spectra, ref_valid):
    local_bins = spectra.shape[1]
    stations = spectra.shape[3]
    sources = ref_spectra.shape[3]
    freq_devs = lax.axis_size("freq")
    pair_devs = lax.axis_size("pair")
    recv_local = stations // (freq_devs * pair_devs)
    before, after = halo_powers(spectra, ref_spectra, "freq")
    valid = valid.astype(jnp.float32)
    ref_valid = ref_valid.astype(jnp.float32)
    pair_count = jnp.dot(valid.T, ref_valid, precision=lax.Precision.HIGHEST)
    if pair_devs == 1:
        scale, dtype = 1.0 / jnp.sqrt(pair_count + 1.0), jnp.bfloat16
    else:
        scale, dtype = jnp.ones_like(pair_count), jnp.float32
    stacked = cross_grams(
        spectra.transpose(1, 2, 0, 3), ref_spectra.transpose(1, 2, 0, 3), before, after, valid, ref_valid, scale, dtype
    )
    if pair_devs > 1:
        stacked = stacked.reshape(freq_devs, pair_devs, recv_local, 2 * local_bins, sources)
        pair_count = pair_count.reshape(freq_devs, pair_devs, recv_local, 1, sources)
        stacked, pair_count = (
            lax.psum_scatter(stacked, "pair", scatter_dimension=1, tiled=True),
            lax.psum_scatter(pair_count, "pair", scatter_dimension=1, tiled=True),
        )
        stacked = (stacked / jnp.sqrt(pair_count + 1.0)).astype(jnp.bfloat16)
    stacked = stacked.reshape(freq_devs, recv_local, 2 * local_bins, sources)
    half_devs = freq_devs // 2
    first_bin = lax.axis_index("freq") // half_devs * (half_devs * local_bins)
    weights = half_table(first_bin, local_bins, half_devs, -(-LAGS // 16) * 16)
    return exchange(stacked, weights).transpose(1, 0, 2)


def solution(mesh):
    placed = (
        P(("grp", "pair"), "freq", None, None),
        P(("grp", "pair"), None),
        P(("grp", "pair"), "freq", None, None),
        P(("grp", "pair"), None),
    )
    return jax.shard_map(
        local,
        mesh=mesh,
        in_specs=placed,
        out_specs=P("grp", ("freq", "pair"), None),
        check_vma=False,
    )
```

```python
import functools
import math

import jax
import jax.numpy as jnp
from jax import lax
from jax.experimental import pallas as pl
from jax.experimental.pallas import tpu as pltpu
from jax.sharding import PartitionSpec as P

F = 1024
LAGS = 401
REACH = 10
LANES = 128
LAG_ROWS = 16


water_level = 0.1


def edge_powers(spectra, ref_spectra, first, width):
    parts = []
    for array in (spectra, ref_spectra):
        edge = lax.slice_in_dim(array, first, first + width, axis=1).transpose(1, 2, 0, 3).astype(jnp.float32)
        parts.append(edge[:, 0] * edge[:, 0] + edge[:, 1] * edge[:, 1])
    return jnp.concatenate(parts, axis=2)


def halo_powers(spectra, ref_spectra, axis):
    count, length = lax.axis_size(axis), spectra.shape[1]
    up = [(i, (i + 1) % count) for i in range(count - 1)]
    down = [(j, i) for i, j in up]
    last = edge_powers(spectra, ref_spectra, length - REACH, REACH)
    first = edge_powers(spectra, ref_spectra, 0, REACH)
    return lax.ppermute(last, axis, up), lax.ppermute(first, axis, down)


def gram_kernel(x_ref, y_ref, before_ref, after_ref, valid_ref, ref_valid_ref, scale_ref, out_ref, power, gram, sem):
    bins = x_ref.shape[0]
    stations = x_ref.shape[3]
    sources = y_ref.shape[3]
    block = out_ref.shape[2]
    step = pl.program_id(0)

    @pl.when(step == 0)
    def _():
        copies = (
            pltpu.make_async_copy(before_ref, power.at[pl.ds(0, REACH)], sem.at[0]),
            pltpu.make_async_copy(after_ref, power.at[pl.ds(REACH + bins, REACH)], sem.at[1]),
        )
        for copy in copies:
            copy.start()

        @pl.loop(0, bins)
        def _(f):
            for ref, columns in ((x_ref, pl.ds(0, stations)), (y_ref, pl.ds(stations, sources))):
                real_part = ref[f, 0].astype(jnp.float32)
                imag_part = ref[f, 1].astype(jnp.float32)
                power[f + REACH, :, columns] = real_part * real_part + imag_part * imag_part

        for copy in copies:
            copy.wait()

        @pl.loop(0, bins + 2 * REACH - 2)
        def _(f):
            power[f] = power[f] + power[f + 1] + power[f + 2]

    @pl.loop(0, block)
    def _(b):
        f = step * block + b
        whites = []
        for ref, mask, columns in (
            (x_ref, valid_ref, pl.ds(0, stations)),
            (y_ref, ref_valid_ref, pl.ds(stations, sources)),
        ):
            smooth = power[f, :, columns]
            for k in range(3, 2 * REACH + 1, 3):
                smooth = smooth + power[f + k, :, columns]
            gain = lax.rsqrt(smooth * (1.0 / (2 * REACH + 1)) + water_level) * mask[...]
            whites.append([ref[f, c].astype(jnp.float32) * gain for c in range(2)])
        (rec_re, rec_im), (ref_re, ref_im) = whites
        rec = jnp.concatenate([rec_re.astype(jnp.bfloat16), rec_im.astype(jnp.bfloat16)], axis=0)
        for c, pieces in enumerate(((ref_re, ref_im), (-ref_im, ref_re))):
            other = jnp.concatenate([piece.astype(jnp.bfloat16) for piece in pieces], axis=0)
            cross = lax.dot_general(rec, other, (((0,), (0,)), ((), ())), preferred_element_type=jnp.float32)
            cross = cross * scale_ref[...]
            for q in range(sources // LANES):
                gram[c * (sources // LANES) + q, pl.ds(pl.multiple_of(b * stations, stations), stations)] = cross[
                    :, q * LANES : (q + 1) * LANES
                ]

    @pl.loop(0, stations, unroll=8)
    def _(j):
        for c in range(2):
            for q in range(sources // LANES):
                rows = gram[c * (sources // LANES) + q, pl.ds(j, block, stride=stations)]
                out_ref[j, c, :, pl.ds(q * LANES, LANES)] = rows.astype(out_ref.dtype)


def cross_grams(spectra, ref_spectra, before, after, valid, ref_valid, scale, dtype):
    bins, parts, windows, stations = spectra.shape
    sources = ref_spectra.shape[3]
    block = 8
    whole = lambda shape: pl.BlockSpec(shape, lambda i: (0,) * len(shape), pipeline_mode=pl.Buffered(1))
    return pl.pallas_call(
        gram_kernel,
        grid=(bins // block,),
        out_shape=jax.ShapeDtypeStruct((stations, 2, bins, sources), dtype),
        in_specs=[
            whole(spectra.shape),
            whole(ref_spectra.shape),
            pl.BlockSpec(memory_space=pl.ANY),
            pl.BlockSpec(memory_space=pl.ANY),
            whole(valid.shape),
            whole(ref_valid.shape),
            whole(scale.shape),
        ],
        out_specs=pl.BlockSpec((stations, 2, block, sources), lambda i: (0, 0, i, 0)),
        scratch_shapes=[
            pltpu.VMEM((bins + 2 * REACH, windows, stations + sources), jnp.float32),
            pltpu.VMEM((2 * sources // LANES, block * stations, LANES), jnp.float32),
            pltpu.SemaphoreType.DMA((2,)),
        ],
        compiler_params=pltpu.CompilerParams(vmem_limit_bytes=60 * 1024 * 1024),
    )(spectra, ref_spectra, before, after, valid, ref_valid, scale)


def lag_rows(first_lag, first_bin, bins, shape):
    column = lax.broadcasted_iota(jnp.int32, shape, 1)
    lag = lax.broadcasted_iota(jnp.int32, shape, 0) + first_lag + (F - (LAGS - 1) // 2)
    bin_index = first_bin + lax.div(column, 2 * bins) * bins + lax.rem(column, bins)
    imag = lax.rem(lax.div(column, bins), 2)
    phases = lax.rem(lag * bin_index, F).astype(jnp.float32) * (2.0 * jnp.pi / F)
    values = jnp.where(imag == 1, -jnp.sin(phases), jnp.cos(phases)) * (1.0 / math.sqrt(F))
    return values.astype(jnp.bfloat16)


def partner_of(device, n):
    quarter = n // 4
    return (3 - lax.div(device, quarter)) * quarter + lax.rem(device, quarter)


def exchange_kernel(n, chunks, x_ref, out_ref, w_ref, buf, part, got, send_sem, recv_sem, part_sem, got_sem, own_sem):
    h = n // 2
    rows_chunk = x_ref.shape[1] // chunks
    depth = h * x_ref.shape[2]
    sources = x_ref.shape[3]
    lags = out_ref.shape[1]
    me = lax.axis_index("freq")
    half = lax.div(me, h)
    pos = lax.rem(me, h)
    base = half * h
    partner = partner_of(me, n)

    def peer_of(k):
        quarter = h // 2
        side = lax.rem(lax.div(pos, quarter) + 1 + lax.div(k, quarter), 2)
        return side * quarter + lax.rem(pos + k + lax.div(k, quarter), quarter)

    barrier = pltpu.get_barrier_semaphore()

    @pl.loop(0, h - 1)
    def _(k):
        pl.semaphore_signal(barrier, inc=1, device_id={"freq": base + peer_of(k)}, device_id_type=pl.DeviceIdType.MESH)

    pl.semaphore_signal(barrier, inc=1, device_id={"freq": partner}, device_id_type=pl.DeviceIdType.MESH)
    pl.semaphore_wait(barrier, h)

    def bins_copy(s, c, k):
        p = peer_of(k)
        rows = pl.ds(c * rows_chunk, rows_chunk)
        return pltpu.make_async_remote_copy(
            src_ref=x_ref.at[partner_of(base + p, n) if s == 0 else base + p, rows],
            dst_ref=buf.at[s, rows, pos],
            send_sem=send_sem.at[s, c, k],
            recv_sem=recv_sem.at[s, c, k],
            device_id={"freq": base + p},
            device_id_type=pl.DeviceIdType.MESH,
        )

    def own_copy(s):
        return pltpu.make_async_copy(x_ref.at[partner if s == 0 else me], buf.at[s, :, pos], own_sem.at[s])

    def sums_copy(c):
        rows = pl.ds(c * rows_chunk, rows_chunk)
        return pltpu.make_async_remote_copy(
            src_ref=part.at[rows],
            dst_ref=got.at[rows],
            send_sem=part_sem.at[c],
            recv_sem=got_sem.at[c],
            device_id={"freq": partner},
            device_id_type=pl.DeviceIdType.MESH,
        )

    def send_bins(s, c):
        @pl.loop(0, h - 1)
        def _(k):
            bins_copy(s, c, k).start()

    def wait_bins(s, c):
        @pl.loop(0, h - 1)
        def _(k):
            bins_copy(s, c, k).wait_recv()

    def to_lags(s, j):
        return jnp.dot(w_ref[...], buf[s, j].reshape(depth, sources), preferred_element_type=jnp.float32)

    own_copy(0).start()
    own_copy(1).start()
    for c in range(chunks):
        send_bins(0, c)

    @pl.loop(0, w_ref.shape[0], step=LAG_ROWS)
    def _(first):
        bins = x_ref.shape[2] // 2
        w_ref[pl.ds(pl.multiple_of(first, LAG_ROWS), LAG_ROWS)] = lag_rows(first, base * bins, bins, (LAG_ROWS, depth))

    own_copy(0).wait()
    for c in range(chunks):
        wait_bins(0, c)

        @pl.loop(c * rows_chunk, (c + 1) * rows_chunk)
        def _(j):
            part[j] = to_lags(0, j).astype(jnp.bfloat16)

        sums_copy(c).start()
        send_bins(1, c)
    own_copy(1).wait()
    for c in range(chunks):
        wait_bins(1, c)
        sums_copy(c).wait_recv()

        @pl.loop(c * rows_chunk, (c + 1) * rows_chunk)
        def _(j):
            total = to_lags(1, j) + got[j].astype(jnp.float32)
            out_ref[j] = total[:lags]

    for c in range(chunks):
        sums_copy(c).wait_send()
        for s in range(2):
            @pl.loop(0, h - 1)
            def _(k):
                bins_copy(s, c, k).wait_send()


def exchange(stacked):
    n, recv_local, depth, sources = stacked.shape
    rows = -(-LAGS // LAG_ROWS) * LAG_ROWS
    h = n // 2
    chunks = math.gcd(recv_local, 8)
    return pl.pallas_call(
        functools.partial(exchange_kernel, n, chunks),
        out_shape=jax.ShapeDtypeStruct((recv_local, LAGS, sources), jnp.float32),
        in_specs=[pl.BlockSpec(memory_space=pl.ANY)],
        out_specs=pl.BlockSpec(memory_space=pltpu.VMEM),
        scratch_shapes=[
            pltpu.VMEM((rows, h * depth), jnp.bfloat16),
            pltpu.VMEM((2, recv_local, h, depth, sources), jnp.bfloat16),
            pltpu.VMEM((recv_local, rows, sources), jnp.bfloat16),
            pltpu.VMEM((recv_local, rows, sources), jnp.bfloat16),
            pltpu.SemaphoreType.DMA((2, chunks, h)),
            pltpu.SemaphoreType.DMA((2, chunks, h)),
            pltpu.SemaphoreType.DMA((chunks,)),
            pltpu.SemaphoreType.DMA((chunks,)),
            pltpu.SemaphoreType.DMA((2,)),
        ],
        compiler_params=pltpu.CompilerParams(collective_id=0, has_side_effects=True, vmem_limit_bytes=56 * 1024 * 1024),
    )(stacked)


def local(spectra, valid, ref_spectra, ref_valid):
    local_bins = spectra.shape[1]
    stations = spectra.shape[3]
    sources = ref_spectra.shape[3]
    freq_devs = lax.axis_size("freq")
    pair_devs = lax.axis_size("pair")
    recv_local = stations // (freq_devs * pair_devs)
    before, after = halo_powers(spectra, ref_spectra, "freq")
    valid = valid.astype(jnp.float32)
    ref_valid = ref_valid.astype(jnp.float32)
    pair_count = jnp.dot(valid.T, ref_valid, precision=lax.Precision.HIGHEST)
    if pair_devs == 1:
        scale, dtype = 1.0 / jnp.sqrt(pair_count + 1.0), jnp.bfloat16
    else:
        scale, dtype = jnp.ones_like(pair_count), jnp.float32
    stacked = cross_grams(
        spectra.transpose(1, 2, 0, 3), ref_spectra.transpose(1, 2, 0, 3), before, after, valid, ref_valid, scale, dtype
    )
    if pair_devs > 1:
        stacked = stacked.reshape(freq_devs, pair_devs, recv_local, 2 * local_bins, sources)
        pair_count = pair_count.reshape(freq_devs, pair_devs, recv_local, 1, sources)
        stacked, pair_count = (
            lax.psum_scatter(stacked, "pair", scatter_dimension=1, tiled=True),
            lax.psum_scatter(pair_count, "pair", scatter_dimension=1, tiled=True),
        )
        stacked = (stacked / jnp.sqrt(pair_count + 1.0)).astype(jnp.bfloat16)
    stacked = stacked.reshape(freq_devs, recv_local, 2 * local_bins, sources)
    return exchange(stacked).transpose(1, 0, 2)


def solution(mesh):
    placed = (
        P(("grp", "pair"), "freq", None, None),
        P(("grp", "pair"), None),
        P(("grp", "pair"), "freq", None, None),
        P(("grp", "pair"), None),
    )
    return jax.shard_map(
        local,
        mesh=mesh,
        in_specs=placed,
        out_specs=P("grp", ("freq", "pair"), None),
        check_vma=False,
    )
```

```python
import functools
import math

import jax
import jax.numpy as jnp
from jax import lax
from jax.experimental import pallas as pl
from jax.experimental.pallas import tpu as pltpu
from jax.sharding import PartitionSpec as P

F = 1024
LAGS = 401
REACH = 10
LANES = 128
LAG_ROWS = 16


water_level = 0.1


def edge_powers(spectra, ref_spectra, first, width):
    parts = []
    for array in (spectra, ref_spectra):
        edge = lax.slice_in_dim(array, first, first + width, axis=1).transpose(1, 2, 0, 3).astype(jnp.float32)
        parts.append(edge[:, 0] * edge[:, 0] + edge[:, 1] * edge[:, 1])
    return jnp.concatenate(parts, axis=2)


def halo_powers(spectra, ref_spectra, axis):
    count, length = lax.axis_size(axis), spectra.shape[1]
    up = [(i, (i + 1) % count) for i in range(count - 1)]
    down = [(j, i) for i, j in up]
    last = edge_powers(spectra, ref_spectra, length - REACH, REACH)
    first = edge_powers(spectra, ref_spectra, 0, REACH)
    return lax.ppermute(last, axis, up), lax.ppermute(first, axis, down)


def gram_kernel(x_ref, y_ref, before_ref, after_ref, valid_ref, ref_valid_ref, scale_ref, out_ref, power, gram, sem):
    bins = x_ref.shape[0]
    stations = x_ref.shape[3]
    sources = y_ref.shape[3]
    block = out_ref.shape[2]
    step = pl.program_id(0)

    @pl.when(step == 0)
    def _():
        copies = (
            pltpu.make_async_copy(before_ref, power.at[pl.ds(0, REACH)], sem.at[0]),
            pltpu.make_async_copy(after_ref, power.at[pl.ds(REACH + bins, REACH)], sem.at[1]),
        )
        for copy in copies:
            copy.start()

        @pl.loop(0, bins)
        def _(f):
            for ref, columns in ((x_ref, pl.ds(0, stations)), (y_ref, pl.ds(stations, sources))):
                real_part = ref[f, 0].astype(jnp.float32)
                imag_part = ref[f, 1].astype(jnp.float32)
                power[f + REACH, :, columns] = real_part * real_part + imag_part * imag_part

        for copy in copies:
            copy.wait()

        @pl.loop(0, bins + 2 * REACH - 2)
        def _(f):
            power[f] = power[f] + power[f + 1] + power[f + 2]

    @pl.loop(0, block)
    def _(b):
        f = step * block + b
        whites = []
        for ref, mask, columns in (
            (x_ref, valid_ref, pl.ds(0, stations)),
            (y_ref, ref_valid_ref, pl.ds(stations, sources)),
        ):
            smooth = power[f, :, columns]
            for k in range(3, 2 * REACH + 1, 3):
                smooth = smooth + power[f + k, :, columns]
            gain = lax.rsqrt(smooth * (1.0 / (2 * REACH + 1)) + water_level) * mask[...]
            whites.append([ref[f, c].astype(jnp.float32) * gain for c in range(2)])
        (rec_re, rec_im), (ref_re, ref_im) = whites
        rec = jnp.concatenate([rec_re.astype(jnp.bfloat16), rec_im.astype(jnp.bfloat16)], axis=0)
        for c, pieces in enumerate(((ref_re, ref_im), (-ref_im, ref_re))):
            other = jnp.concatenate([piece.astype(jnp.bfloat16) for piece in pieces], axis=0)
            cross = lax.dot_general(rec, other, (((0,), (0,)), ((), ())), preferred_element_type=jnp.float32)
            cross = cross * scale_ref[...]
            for q in range(sources // LANES):
                gram[c * (sources // LANES) + q, pl.ds(pl.multiple_of(b * stations, stations), stations)] = cross[
                    :, q * LANES : (q + 1) * LANES
                ]

    @pl.loop(0, stations, unroll=8)
    def _(j):
        for c in range(2):
            for q in range(sources // LANES):
                rows = gram[c * (sources // LANES) + q, pl.ds(j, block, stride=stations)]
                out_ref[j, c, :, pl.ds(q * LANES, LANES)] = rows.astype(out_ref.dtype)


def cross_grams(spectra, ref_spectra, before, after, valid, ref_valid, scale, dtype):
    bins, parts, windows, stations = spectra.shape
    sources = ref_spectra.shape[3]
    block = 8
    whole = lambda shape: pl.BlockSpec(shape, lambda i: (0,) * len(shape), pipeline_mode=pl.Buffered(1))
    return pl.pallas_call(
        gram_kernel,
        grid=(bins // block,),
        out_shape=jax.ShapeDtypeStruct((stations, 2, bins, sources), dtype),
        in_specs=[
            whole(spectra.shape),
            whole(ref_spectra.shape),
            pl.BlockSpec(memory_space=pl.ANY),
            pl.BlockSpec(memory_space=pl.ANY),
            whole(valid.shape),
            whole(ref_valid.shape),
            whole(scale.shape),
        ],
        out_specs=pl.BlockSpec((stations, 2, block, sources), lambda i: (0, 0, i, 0)),
        scratch_shapes=[
            pltpu.VMEM((bins + 2 * REACH, windows, stations + sources), jnp.float32),
            pltpu.VMEM((2 * sources // LANES, block * stations, LANES), jnp.float32),
            pltpu.SemaphoreType.DMA((2,)),
        ],
        compiler_params=pltpu.CompilerParams(vmem_limit_bytes=60 * 1024 * 1024),
    )(spectra, ref_spectra, before, after, valid, ref_valid, scale)


def lag_rows(first_lag, first_bin, bins, shape):
    column = lax.broadcasted_iota(jnp.int32, shape, 1)
    lag = lax.broadcasted_iota(jnp.int32, shape, 0) + first_lag + (F - (LAGS - 1) // 2)
    bin_index = first_bin + lax.div(column, 2 * bins) * bins + lax.rem(column, bins)
    imag = lax.rem(lax.div(column, bins), 2)
    phases = lax.rem(lag * bin_index, F).astype(jnp.float32) * (2.0 * jnp.pi / F)
    values = jnp.where(imag == 1, -jnp.sin(phases), jnp.cos(phases)) * (1.0 / math.sqrt(F))
    return values.astype(jnp.bfloat16)


def partner_of(device, n):
    quarter = n // 4
    return (3 - lax.div(device, quarter)) * quarter + lax.rem(device, quarter)


def exchange_kernel(n, chunks, x_ref, out_ref, w_ref, buf, part, got, send_sem, recv_sem, part_sem, got_sem, own_sem):
    h = n // 2
    rows_chunk = x_ref.shape[1] // chunks
    depth = h * x_ref.shape[2]
    sources = x_ref.shape[3]
    lags = out_ref.shape[1]
    me = lax.axis_index("freq")
    half = lax.div(me, h)
    pos = lax.rem(me, h)
    base = half * h
    partner = partner_of(me, n)

    def peer_of(k):
        quarter = h // 2
        side = lax.rem(lax.div(pos, quarter) + 1 + lax.div(k, quarter), 2)
        return side * quarter + lax.rem(pos + k + lax.div(k, quarter), quarter)

    barrier = pltpu.get_barrier_semaphore()

    @pl.loop(0, h - 1)
    def _(k):
        pl.semaphore_signal(barrier, inc=1, device_id={"freq": base + peer_of(k)}, device_id_type=pl.DeviceIdType.MESH)

    pl.semaphore_signal(barrier, inc=1, device_id={"freq": partner}, device_id_type=pl.DeviceIdType.MESH)
    pl.semaphore_wait(barrier, h)

    def bins_copy(s, c, k):
        p = peer_of(k)
        rows = pl.ds(c * rows_chunk, rows_chunk)
        return pltpu.make_async_remote_copy(
            src_ref=x_ref.at[partner_of(base + p, n) if s == 0 else base + p, rows],
            dst_ref=buf.at[s, rows, pos],
            send_sem=send_sem.at[s, c, k],
            recv_sem=recv_sem.at[s, c, k],
            device_id={"freq": base + p},
            device_id_type=pl.DeviceIdType.MESH,
        )

    def own_copy(s):
        return pltpu.make_async_copy(x_ref.at[partner if s == 0 else me], buf.at[s, :, pos], own_sem.at[s])

    def sums_copy(c):
        rows = pl.ds(c * rows_chunk, rows_chunk)
        return pltpu.make_async_remote_copy(
            src_ref=part.at[rows],
            dst_ref=got.at[rows],
            send_sem=part_sem.at[c],
            recv_sem=got_sem.at[c],
            device_id={"freq": partner},
            device_id_type=pl.DeviceIdType.MESH,
        )

    def send_bins(s, c):
        @pl.loop(0, h - 1)
        def _(k):
            bins_copy(s, c, k).start()

    def wait_bins(s, c):
        @pl.loop(0, h - 1)
        def _(k):
            bins_copy(s, c, k).wait_recv()

    def to_lags(s, j):
        return jnp.dot(w_ref[...], buf[s, j].reshape(depth, sources), preferred_element_type=jnp.float32)

    own_copy(0).start()
    own_copy(1).start()
    for c in range(chunks):
        send_bins(0, c)

    @pl.loop(0, w_ref.shape[0], step=LAG_ROWS)
    def _(first):
        bins = x_ref.shape[2] // 2
        w_ref[pl.ds(pl.multiple_of(first, LAG_ROWS), LAG_ROWS)] = lag_rows(first, base * bins, bins, (LAG_ROWS, depth))

    own_copy(0).wait()
    for c in range(chunks):
        wait_bins(0, c)

        @pl.loop(c * rows_chunk, (c + 1) * rows_chunk)
        def _(j):
            part[j] = to_lags(0, j).astype(jnp.bfloat16)

        sums_copy(c).start()
        send_bins(1, c)
    own_copy(1).wait()
    for c in range(chunks):
        wait_bins(1, c)
        sums_copy(c).wait_recv()

        @pl.loop(c * rows_chunk, (c + 1) * rows_chunk)
        def _(j):
            total = to_lags(1, j) + got[j].astype(jnp.float32)
            out_ref[j] = total[:lags]

    for c in range(chunks):
        sums_copy(c).wait_send()
        for s in range(2):
            @pl.loop(0, h - 1)
            def _(k):
                bins_copy(s, c, k).wait_send()


def exchange(stacked):
    n, recv_local, depth, sources = stacked.shape
    rows = -(-LAGS // LAG_ROWS) * LAG_ROWS
    h = n // 2
    chunks = math.gcd(recv_local, 4)
    return pl.pallas_call(
        functools.partial(exchange_kernel, n, chunks),
        out_shape=jax.ShapeDtypeStruct((recv_local, LAGS, sources), jnp.float32),
        in_specs=[pl.BlockSpec(memory_space=pl.ANY)],
        out_specs=pl.BlockSpec(memory_space=pltpu.VMEM),
        scratch_shapes=[
            pltpu.VMEM((rows, h * depth), jnp.bfloat16),
            pltpu.VMEM((2, recv_local, h, depth, sources), jnp.bfloat16),
            pltpu.VMEM((recv_local, rows, sources), jnp.bfloat16),
            pltpu.VMEM((recv_local, rows, sources), jnp.bfloat16),
            pltpu.SemaphoreType.DMA((2, chunks, h)),
            pltpu.SemaphoreType.DMA((2, chunks, h)),
            pltpu.SemaphoreType.DMA((chunks,)),
            pltpu.SemaphoreType.DMA((chunks,)),
            pltpu.SemaphoreType.DMA((2,)),
        ],
        compiler_params=pltpu.CompilerParams(collective_id=0, has_side_effects=True, vmem_limit_bytes=56 * 1024 * 1024),
    )(stacked)


def local(spectra, valid, ref_spectra, ref_valid):
    local_bins = spectra.shape[1]
    stations = spectra.shape[3]
    sources = ref_spectra.shape[3]
    freq_devs = lax.axis_size("freq")
    pair_devs = lax.axis_size("pair")
    recv_local = stations // (freq_devs * pair_devs)
    before, after = halo_powers(spectra, ref_spectra, "freq")
    valid = valid.astype(jnp.float32)
    ref_valid = ref_valid.astype(jnp.float32)
    pair_count = jnp.dot(valid.T, ref_valid, precision=lax.Precision.HIGHEST)
    if pair_devs == 1:
        scale, dtype = 1.0 / jnp.sqrt(pair_count + 1.0), jnp.bfloat16
    else:
        scale, dtype = jnp.ones_like(pair_count), jnp.float32
    stacked = cross_grams(
        spectra.transpose(1, 2, 0, 3), ref_spectra.transpose(1, 2, 0, 3), before, after, valid, ref_valid, scale, dtype
    )
    if pair_devs > 1:
        stacked = stacked.reshape(freq_devs, pair_devs, recv_local, 2 * local_bins, sources)
        pair_count = pair_count.reshape(freq_devs, pair_devs, recv_local, 1, sources)
        stacked, pair_count = (
            lax.psum_scatter(stacked, "pair", scatter_dimension=1, tiled=True),
            lax.psum_scatter(pair_count, "pair", scatter_dimension=1, tiled=True),
        )
        stacked = (stacked / jnp.sqrt(pair_count + 1.0)).astype(jnp.bfloat16)
    stacked = stacked.reshape(freq_devs, recv_local, 2 * local_bins, sources)
    return exchange(stacked).transpose(1, 0, 2)


def solution(mesh):
    placed = (
        P(("grp", "pair"), "freq", None, None),
        P(("grp", "pair"), None),
        P(("grp", "pair"), "freq", None, None),
        P(("grp", "pair"), None),
    )
    return jax.shard_map(
        local,
        mesh=mesh,
        in_specs=placed,
        out_specs=P("grp", ("freq", "pair"), None),
        check_vma=False,
    )
```
